32 devices in a mesh: tp: 2 (over core), ep: 16 (over z, y, x).
Axes of the slice: x: 2, y: 2, z: 4, core: 2. Of those that a mesh axis runs over, the one named last changes fastest.
Arguments:
- tokens: bfloat16 [2048, 4096], P('ep', 'tp'), may hold values from -6 to 6
- expert_ids: int32 [2048, 8], P('ep'), may hold values from 0 to 15, all different within a row; in each aligned block of 128 rows (0 to 127, 128 to 255, ...) at most 128 rows name the same one
- route_weights: float32 [2048, 8], P('ep'), may hold values from 0.1 to 1
- gate_weight: bfloat16 [16, 4096, 1536], P('ep', None, 'tp'), may hold values from -0.09375 to 0.09375
- up_weight: bfloat16 [16, 4096, 1536], P('ep', None, 'tp'), may hold values from -0.09375 to 0.09375
- down_weight: bfloat16 [16, 1536, 4096], P('ep', 'tp'), may hold values from -0.15625 to 0.15625
- value_weight: float32 [4096], P('tp'), may hold values from -0.375 to 0.375
- sequence_ids: int32 [16, 128], P('ep'), may hold values from 0 to 3, never falling along the last dimension, each value on 1 to 64 neighbouring positions
Outputs:
- layer_output: bfloat16 [2048, 4096], P('ep', 'tp')
- rewards: float32 [16, 4], P('ep')
The draws below stay inside these ranges and needn't reach their ends.
Inputs may be any that keep to these rules, and one draw needn't show every extreme that they name: `expert_ids`: each token names 8 different experts. Within each group's 128 rows no expert is named more than 128 times, a bound that some block reaches. `sequence_ids`: within each group the ids never fall, every one of the 4 ids occurs, and the longest sequence has exactly 64 tokens.
All inputs are finite; a program needn't handle non-finite values.
Results may differ from the reference program's by a relative error of at most 0.0095.
Values may be sent and summed in bfloat16 or wider, within the bound.
A program may use at most 128 MiB of HBM per device.

```python
import math
import jax
import jax.numpy as jnp
import numpy as np
from jax import lax

D = 4096
FF = 1536
TOP = 8
TOK_GRP = 128
SEQ_GRP = 4
GROUPS = 16
EXPERTS = 16
CAP = 128
TOKENS = 2048
N_TP = 2


def block_levels(own_key, dims, cuts, least, top_value):
    def one(dim, parts):
        heights = jax.random.uniform(jax.random.fold_in(jax.random.fold_in(own_key, 6), dim), (parts,), jnp.float32, least / len(cuts), top_value / len(cuts))
        return jnp.repeat(jnp.exp(heights), dims[dim] // parts).reshape((-1,) + (1,) * (len(dims) - dim - 1))

    factor_of = one(*cuts[0])
    for cut in cuts[1:]:
        factor_of = factor_of * one(*cut)
    return factor_of


def length_profile(count, total, most, slope):
    portions = [(1 << 20) // math.isqrt(standing ** slope) + 1 for standing in range(2, count + 1)]
    surplus, given = total - most - (count - 1), [1] * (count - 1)
    while surplus > 0:
        free = [i for i in range(count - 1) if given[i] < most]
        mass, budget = sum([portions[i] for i in free]), surplus
        for i in free:
            addition = min(most - given[i], max(1, budget * portions[i] // mass), surplus)
            given[i] = given[i] + addition
            surplus = surplus - addition
    return np.array([most] + given)


def ragged_sizes(own_key, number_of, total, most, lean):
    if number_of == 2:
        one = jax.random.randint(own_key, (), max(1, total - most), min(most, total - 1) + 1)
        return jnp.stack([one, total - one])
    lengths = jnp.asarray(length_profile(number_of, total, most, lean), jnp.int32)
    pairs = (number_of - 1) // 2
    giver, receiver = lengths[1:1 + 2 * pairs:2], lengths[2:2 + 2 * pairs:2]
    room = jnp.minimum(giver - 1, most - receiver)
    moved = jax.random.randint(jax.random.fold_in(own_key, 1), (pairs,), 0, 1 << 20) % (room + 1)
    lengths = lengths.at[1:1 + 2 * pairs:2].set(giver - moved).at[2:2 + 2 * pairs:2].set(receiver + moved)
    return lengths[jax.random.permutation(jax.random.fold_in(own_key, 2), number_of)]


def routed_block(key, own, number, rows, count, top, bound, lean):
    sequence = jax.random.permutation(key, count)
    heavy_load, usual = shares(count, rows * top, bound, lean, True), shares(count, rows * top, bound, lean, False)
    places = jnp.arange(count)

    def named(tallies, turn):
        used = int((tallies > 0).sum())
        fixed = max(1, used // 4)
        passed = fixed + (places - fixed + turn * (used - fixed)) % max(1, count - fixed)
        return jnp.zeros((count,), jnp.int32).at[sequence[jnp.where(places < fixed, places, passed)]].set(jnp.asarray(tallies, jnp.int32))

    tallies = jnp.where(number % 4 == 0, named(heavy_load, number // 4), named(usual, number - number // 4 - 1))
    mixed = jax.random.permutation(jax.random.fold_in(own, 3), count)
    donor, receiver = mixed[0:count // 2 * 2:2], mixed[1:count // 2 * 2:2]
    slack = jnp.minimum(tallies[donor] - 1, bound - tallies[receiver]) // 2
    slack = jnp.where((donor == sequence[0]) | (receiver == sequence[0]) | (tallies[receiver] == 0), 0, jnp.maximum(slack, 0))
    passed = jax.random.randint(jax.random.fold_in(own, 4), (count // 2,), 0, 1 << 20) % (slack + 1)
    tallies = tallies.at[donor].add(-passed).at[receiver].add(passed)
    labels = jnp.searchsorted(jnp.cumsum(tallies), jnp.arange(rows * top), side="right").astype(jnp.int32)
    grid = labels.reshape(top, rows).T
    grid = grid[jax.random.permutation(jax.random.fold_in(own, 1), rows)]
    turn = jax.random.randint(jax.random.fold_in(own, 2), (rows, 1), 0, top)
    return jnp.take_along_axis(grid, (jnp.arange(top)[None, :] + turn) % top, axis=1)


def shares(number_of, total, most, slope, full):
    loads = [(1 << 20) // math.isqrt(grade ** slope) + 1 for grade in range(1, number_of + 1)]
    largest = most if full else min(most, max(-(-total // number_of), total * loads[0] // sum(loads)))
    least = 1 if total - largest >= number_of - 1 else 0
    holding, rest = [largest] + [least] * (number_of - 1), total - largest - least * (number_of - 1)
    while rest > 0:
        movable = [i for i in range(1, number_of) if holding[i] < largest] or [i for i in range(1, number_of) if holding[i] < most]
        pool, budget = sum([loads[i] for i in movable]), rest
        for i in movable:
            addition = min(most - holding[i], max(1, budget * loads[i] // pool), rest)
            holding[i] = holding[i] + addition
            rest = rest - addition
    return np.array(holding)


def noise(stream_key, shape, width, most, cuts=(), kind=jnp.bfloat16):
    array = width * jax.random.normal(stream_key, shape, jnp.float32)
    if cuts:
        array = array * block_levels(stream_key, shape, cuts, -0.22, 0.18)
    return jnp.clip(array, -most, most).astype(kind)


def setup_inputs(seed: int = 0) -> dict:
    key_list = jax.random.split(jax.random.key(seed), 9)
    tokens = noise(key_list[0], (TOKENS, D), 1.0, 6.0, ((0, 16), (1, 2)))
    expert_ids_keys = jax.random.split(jax.random.fold_in(key_list[1], 1), TOKENS // TOK_GRP)
    expert_ids_turns = jax.random.permutation(jax.random.fold_in(key_list[1], 3), TOKENS // TOK_GRP)
    expert_ids = jax.vmap(lambda own, number: routed_block(jax.random.fold_in(key_list[1], 2), own, number, TOK_GRP, EXPERTS, TOP, CAP, 2))(expert_ids_keys, expert_ids_turns).reshape((TOKENS, TOP))
    route_weights = jnp.clip(jnp.exp(math.log(1.0) - 2.3025851 * jax.random.uniform(key_list[2], (TOKENS, TOP), jnp.float32) ** block_levels(key_list[2], (TOKENS, TOP), ((0, 16),), -0.2, 0.2)), 0.1, 1.0)
    gate_weight = noise(key_list[3], (EXPERTS, D, FF), D ** -0.5, 0.09375, ((0, 16), (2, 2)))
    up_weight = noise(key_list[4], (EXPERTS, D, FF), D ** -0.5, 0.09375, ((0, 16), (2, 2)))
    down_weight = noise(key_list[5], (EXPERTS, FF, D), FF ** -0.5, 0.15625, ((0, 16), (1, 2)))
    value_weight = noise(key_list[6], (D,), (D // 16) ** -0.5, 0.375, ((0, 2),), jnp.float32)
    sequence_ids = jax.vmap(lambda own: jnp.searchsorted(jnp.cumsum(ragged_sizes(own, SEQ_GRP, TOK_GRP, TOK_GRP // 2, 0)), jnp.arange(TOK_GRP), side="right"))(jax.random.split(key_list[7], GROUPS)).reshape((GROUPS, TOK_GRP)).astype(jnp.int32)
    return {"tokens": tokens, "expert_ids": expert_ids, "route_weights": route_weights, "gate_weight": gate_weight, "up_weight": up_weight, "down_weight": down_weight, "value_weight": value_weight, "sequence_ids": sequence_ids}


def slot_tables(route_ids, experts, capacity):
    tok_count, top_count = route_ids.shape
    flat_ids = route_ids.reshape(tok_count * top_count).astype(jnp.int32)
    one_hot = (flat_ids[:, None] == jnp.arange(experts, dtype=jnp.int32)[None, :]).astype(jnp.int32)
    before = jnp.cumsum(one_hot, axis=0, dtype=jnp.int32) - one_hot
    position = lax.optimization_barrier(jnp.sum(before * one_hot, axis=1, dtype=jnp.int32))
    slot_index = (flat_ids * capacity + position).astype(jnp.int32)
    pair_token = (jnp.arange(tok_count * top_count, dtype=jnp.int32) // top_count).astype(jnp.int32)
    owner_token = jnp.zeros((experts * capacity,), jnp.int32).at[slot_index].set(pair_token)
    filled = jnp.zeros((experts * capacity,), jnp.int32).at[slot_index].set(1)
    return (slot_index.reshape(tok_count, top_count), owner_token, filled)

def expert_apply(operands):
    rows_in, gate_mat, up_mat, down_mat = operands
    gate = jnp.dot(rows_in, gate_mat, preferred_element_type=jnp.float32)
    upper = jnp.dot(rows_in, up_mat, preferred_element_type=jnp.float32)
    hidden = (jax.nn.silu(gate) * upper).astype(jnp.bfloat16)
    quarter = FF // N_TP
    total = jnp.zeros((rows_in.shape[0], D), jnp.float32)
    for index in range(N_TP):
        part_sum = jnp.dot(hidden[:, index * quarter:(index + 1) * quarter], down_mat[index * quarter:(index + 1) * quarter], preferred_element_type=jnp.float32)
        total = total + part_sum.astype(jnp.bfloat16).astype(jnp.float32)
    return total.astype(jnp.bfloat16)

def reference(tokens, expert_ids, route_weights, gate_weight, up_weight, down_weight, value_weight, sequence_ids):
    ids_grouped = expert_ids.reshape(GROUPS, TOK_GRP, TOP)
    slot_index, owner_token, filled = jax.vmap(lambda ids: slot_tables(ids, EXPERTS, CAP))(ids_grouped)
    token_blocks = tokens.reshape(GROUPS, TOK_GRP, D)

    def build(block, owners, live):
        return block[owners] * live.astype(jnp.bfloat16)[:, None]
    outgoing = jax.vmap(build)(token_blocks, owner_token, filled)
    per_expert = outgoing.reshape(GROUPS, EXPERTS, CAP, D).transpose(1, 0, 2, 3).reshape(EXPERTS, GROUPS * CAP, D)
    results = lax.map(expert_apply, (per_expert, gate_weight, up_weight, down_weight))
    back_rows = results.reshape(EXPERTS, GROUPS, CAP, D).transpose(1, 0, 2, 3).reshape(GROUPS, EXPERTS * CAP, D)
    picked = jax.vmap(lambda rows_back, slots: rows_back[slots])(back_rows, slot_index)
    weights_grouped = route_weights.reshape(GROUPS, TOK_GRP, TOP).astype(jnp.float32)
    share = weights_grouped / lax.optimization_barrier(jnp.sum(weights_grouped, axis=2, keepdims=True))
    combined = token_blocks.astype(jnp.float32) + jnp.einsum('gtk,gtkd->gtd', share, picked.astype(jnp.float32))
    layer_output = combined.astype(jnp.bfloat16)
    as_float = layer_output.astype(jnp.float32)
    squares = lax.optimization_barrier(jnp.sum(as_float * as_float, axis=2))
    along = lax.optimization_barrier(jnp.sum(as_float * value_weight.astype(jnp.float32)[None, None, :], axis=2))
    values = along * lax.rsqrt(squares / D + 1e-06)
    members = (sequence_ids[:, None, :] == jnp.arange(SEQ_GRP, dtype=jnp.int32)[None, :, None]).astype(jnp.float32)
    sums = lax.optimization_barrier(jnp.sum(members * values[:, None, :], axis=2))
    counts = lax.optimization_barrier(jnp.sum(members, axis=2))
    rewards = sums / counts
    return (layer_output.reshape(TOKENS, D), rewards)
```

```python
import jax
import jax.numpy as jnp
from jax import lax
from jax.experimental import pallas as pl
from jax.experimental.pallas import tpu as pltpu
from jax.sharding import PartitionSpec as P

SEQ_GRP = 4
CHUNKS = 1


def head(layer_output, value_weight, sequence_ids, parts):
    width_part = layer_output.shape[1]
    as_float = layer_output.astype(jnp.float32)
    squares = jnp.sum(as_float * as_float, axis=1)
    along = jnp.sum(as_float * value_weight[None, :], axis=1)
    squares, along = lax.psum((squares, along), "tp")
    values = along * lax.rsqrt(squares / (width_part * parts) + 1e-06)
    members = (sequence_ids[0][None, :] == jnp.arange(SEQ_GRP, dtype=jnp.int32)[:, None]).astype(
        jnp.float32
    )
    sums = jnp.sum(members * values[None, :], axis=1)
    counts = jnp.sum(members, axis=1)
    rewards = sums / counts
    return rewards[None, :]


def plain_shards(
    tokens,
    expert_ids,
    route_weights,
    gate_weight,
    up_weight,
    down_weight,
    value_weight,
    sequence_ids,
):
    tok_count, width_part = tokens.shape
    groups = lax.axis_size("ep")
    parts = lax.axis_size("tp")
    share = route_weights / jnp.sum(route_weights, axis=1, keepdims=True)
    named = expert_ids[:, :, None] == jnp.arange(groups, dtype=jnp.int32)[None, None, :]
    dense = jnp.sum(jnp.where(named, share[:, :, None], 0.0), axis=1)
    dense_all = lax.all_gather(dense, "ep", axis=0)
    mine = lax.dynamic_index_in_dim(dense_all, lax.axis_index("ep"), 2, keepdims=False)
    gate_local = gate_weight[0].reshape(parts, width_part, -1)
    up_local = up_weight[0].reshape(parts, width_part, -1)
    rows = tok_count // CHUNKS
    pieces = []
    for c in range(CHUNKS):
        own = tokens[c * rows:(c + 1) * rows]
        half = lax.all_gather(own, "ep", axis=0, tiled=True)
        full = lax.all_gather(half, "tp", axis=0)
        gate = jnp.einsum("qtd,qdf->tf", full, gate_local, preferred_element_type=jnp.float32)
        upper = jnp.einsum("qtd,qdf->tf", full, up_local, preferred_element_type=jnp.float32)
        scale = mine[:, c * rows:(c + 1) * rows].reshape(groups * rows, 1)
        hidden = (jax.nn.silu(gate) * upper).astype(jnp.bfloat16)
        terms = jnp.dot(hidden, down_weight[0], preferred_element_type=jnp.float32)
        terms = (terms * scale).astype(jnp.bfloat16)
        summed = lax.psum_scatter(terms, "tp", scatter_dimension=1, tiled=True)
        pieces.append(lax.psum_scatter(summed, "ep", scatter_dimension=0, tiled=True))
    routed = jnp.concatenate(pieces, axis=0).astype(jnp.float32)
    layer_output = (tokens.astype(jnp.float32) + routed).astype(jnp.bfloat16)
    return (layer_output, head(layer_output, value_weight, sequence_ids, parts))


MESH = pl.DeviceIdType.MESH
GRP = 128
PAD = 128


def fused(
    tok, gate_hbm, up_hbm, down_hbm, out,
    held, gate_w, up_w, down_w, hid, scale, part, s_in, f_in, z_in,
    w_sem, az_s, az_r, af_s, af_r, as_s, as_r, at_s, at_r,
    rt_s, rt_r, rs_s, rs_r, rf_s, rf_r, rz_s, rz_r,
):
    half = out.shape[1]
    t = lax.axis_index("tp")
    e = lax.axis_index("ep")
    x = lax.rem(e, 2)
    y = lax.rem(lax.div(e, 2), 2)
    z = lax.div(e, 4)
    l_own = lax.rem(e, 4)
    l_x = l_own + 1 - 2 * x
    l_y = l_own + 2 - 4 * y
    l_diag = 3 - l_own
    e_x = e + 1 - 2 * x
    e_y = e + 2 - 4 * y
    e_f = e_y * (1 - t) + e_x * t
    e_s = e_x * (1 - t) + e_y * t
    l_f = l_y * (1 - t) + l_x * t
    l_s = l_x * (1 - t) + l_y * t
    lines = (l_own, l_x, l_y, l_diag)
    i_f = 2 - t
    i_s = 1 + t
    near = (t, e_f)
    far = (t, e_s)
    twin = (1 - t, e)

    def peer(d):
        return (t, lax.rem(z + d, 4) * 4 + l_own)

    def span(d):
        return pl.ds(pl.multiple_of(lax.rem(z - d + 4, 4) * GRP, GRP), GRP)

    def remote(src, dst, send, recv, target):
        return pltpu.make_async_remote_copy(
            src_ref=src, dst_ref=dst, send_sem=send, recv_sem=recv,
            device_id=target, device_id_type=MESH,
        )

    loads = [
        pltpu.make_async_copy(a, b, w_sem.at[i])
        for i, (a, b) in enumerate(((gate_hbm, gate_w), (up_hbm, up_w), (down_hbm, down_w)))
    ]
    for load in loads:
        load.start()

    barrier = pltpu.get_barrier_semaphore()
    for target in (peer(1), peer(2), peer(3), near, far, twin):
        pl.semaphore_signal(barrier, inc=1, device_id=target, device_id_type=MESH)
    pl.semaphore_wait(barrier, 6)

    def own_block(d):
        return tok if d == 0 else held.at[t, l_own, span(d)]

    def z_copy(d):
        return remote(tok, held.at[t, l_own, span(0)], az_s.at[d - 1], az_r.at[d - 1], peer(d))

    def f_copy(d):
        return remote(own_block(d), held.at[t, l_own, span(d)], af_s.at[d], af_r.at[d], near)

    def s_copy(k, d):
        line = l_own if k == 0 else l_f
        src = own_block(d) if k == 0 else held.at[t, line, span(d)]
        return remote(src, held.at[t, line, span(d)], as_s.at[k, d], as_r.at[k, d], far)

    def t_copy(i, line, d, src=None):
        src = held.at[t, line, span(d)] if src is None else src
        return remote(src, held.at[t, line, span(d)], at_s.at[i, d], at_r.at[i, d], twin)

    def arrived(line, d, sem, core=None):
        ref = held.at[t if core is None else core, line, span(d)]
        remote(ref, ref, w_sem.at[0], sem, twin).wait_recv()

    sent = []

    def go(copy):
        copy.start()
        sent.append(copy)

    for d in (1, 3, 2):
        go(z_copy(d))
    go(f_copy(0))
    go(s_copy(0, 0))
    go(t_copy(0, l_own, 0, tok))
    held[t, l_own, span(0)] = tok[...]
    for d in (0, 1, 3, 2):
        if d:
            arrived(l_own, d, az_r.at[d - 1])
            go(f_copy(d))
            go(s_copy(0, d))
            go(t_copy(0, l_own, d))
        arrived(l_f, d, af_r.at[d])
        go(s_copy(1, d))
        go(t_copy(i_f, l_f, d))

    def expert(i):
        line = lines[i]
        for d in range(4):
            arrived(line, d, at_r.at[i, d], 1 - t)
        lane = lax.broadcasted_iota(jnp.int32, (4 * GRP, PAD), 1)
        shares = held[t, line, :, pl.ds(half, PAD)].astype(jnp.float32)
        scale[...] = jnp.sum(jnp.where(lax.rem(lane, 16) == e, shares, 0.0), axis=1, keepdims=True)

        def hidden(n, carry):
            cols = pl.ds(pl.multiple_of(n * 256, 256), 256)
            a = held[0, line, :, pl.ds(0, half)]
            b = held[1, line, :, pl.ds(0, half)]
            f32 = jnp.float32
            g = jnp.dot(a, gate_w[pl.ds(0, half), cols], preferred_element_type=f32)
            g += jnp.dot(b, gate_w[pl.ds(half, half), cols], preferred_element_type=f32)
            u = jnp.dot(a, up_w[pl.ds(0, half), cols], preferred_element_type=f32)
            u += jnp.dot(b, up_w[pl.ds(half, half), cols], preferred_element_type=f32)
            hid[:, cols] = (g / (1.0 + jnp.exp(-g)) * u * scale[...]).astype(jnp.bfloat16)
            return carry

        lax.fori_loop(0, hid.shape[1] // 256, hidden, 0)

        def term(n, core):
            cols = pl.ds(pl.multiple_of(core * half + n * 256, 256), 256)
            return jnp.dot(hid[...], down_w[:, cols], preferred_element_type=jnp.float32)

        def swap(c):
            cols = pl.ds(c * (half // 2), half // 2)
            return remote(
                held.at[1 - t, line, :, cols], part.at[i, :, cols],
                rt_s.at[i, c], rt_r.at[i, c], twin,
            )

        steps = half // 512
        for c in range(2):
            def other(n, carry):
                cols = pl.ds(pl.multiple_of(n * 256, 256), 256)
                held[1 - t, line, :, cols] = term(n, 1 - t).astype(jnp.bfloat16)
                return carry

            lax.fori_loop(c * steps, (c + 1) * steps, other, 0)
            go(swap(c))
        for c in range(2):
            swap(c).wait_recv()

            def mine(n, carry):
                cols = pl.ds(pl.multiple_of(n * 256, 256), 256)
                total = term(n, t) + part[i, :, cols].astype(jnp.float32)
                part[i, :, cols] = total.astype(jnp.bfloat16)
                return carry

            lax.fori_loop(c * steps, (c + 1) * steps, mine, 0)

    def rs_copy(k, d):
        i = i_s if k == 0 else 3
        return remote(part.at[i, span(d)], s_in.at[k, span(d)], rs_s.at[k, d], rs_r.at[k, d], far)

    def send_far(k):
        for d in (1, 3, 2, 0):
            rs_copy(k, d).start()

    for load in loads:
        load.wait()
    expert(0)
    for d in (0, 1, 3, 2):
        arrived(l_s, d, as_r.at[0, d])
        go(t_copy(i_s, l_s, d))
    expert(1)
    pl.when(t == 0)(lambda: send_far(0))
    for d in (0, 1, 3, 2):
        arrived(l_diag, d, as_r.at[1, d])
        go(t_copy(3, l_diag, d))
    expert(2)
    pl.when(t == 1)(lambda: send_far(0))
    expert(3)
    send_far(1)

    def add(dst, row, *others):
        def chunk(r, carry):
            at = pl.ds(pl.multiple_of(row + r * 16, 16), 16)
            total = dst[at].astype(jnp.float32)
            for other in others:
                total += other[at].astype(jnp.float32)
            dst[at] = total.astype(jnp.bfloat16)
            return carry

        lax.fori_loop(0, GRP // 16, chunk, 0)

    def start_row(d):
        return lax.rem(z - d + 4, 4) * GRP

    def rf_copy(d):
        return remote(part.at[i_f, span(d)], f_in.at[span(d)], rf_s.at[d], rf_r.at[d], near)

    def rz_copy(d):
        return remote(
            part.at[0, span(d)], z_in.at[d - 1], rz_s.at[d - 1], rz_r.at[d - 1], peer(4 - d)
        )

    for d in (1, 3, 2, 0):
        rs_copy(1, d).wait_recv()
        add(part.at[i_f], start_row(d), s_in.at[1])
        go(rf_copy(d))
    for d in (1, 3, 2, 0):
        rs_copy(0, d).wait_recv()
        rf_copy(d).wait_recv()
        add(part.at[0], start_row(d), s_in.at[0], f_in)
        if d:
            go(rz_copy(d))
    for d in (1, 3, 2):
        rz_copy(d).wait_recv()

    def last(r, carry):
        at = pl.ds(pl.multiple_of(r * 16, 16), 16)
        total = part[0, pl.ds(pl.multiple_of(z * GRP + r * 16, 16), 16)].astype(jnp.float32)
        for k in range(3):
            total += z_in[k, at].astype(jnp.float32)
        total += tok[at, pl.ds(0, half)].astype(jnp.float32)
        out[at] = total.astype(jnp.bfloat16)
        return carry

    lax.fori_loop(0, GRP // 16, last, 0)
    for copy in sent:
        copy.wait_send()
    for k in range(2):
        for d in range(4):
            rs_copy(k, d).wait_send()


def routed_layer(block, gate, up, down):
    half = block.shape[1] - PAD
    width, units = gate.shape
    bf16 = jnp.bfloat16
    dma = pltpu.SemaphoreType.DMA
    flops = 2 * 16 * GRP * 3 * width * units
    return pl.pallas_call(
        fused,
        out_shape=jax.ShapeDtypeStruct((GRP, half), bf16),
        in_specs=[pl.BlockSpec(memory_space=pltpu.VMEM)] + [pl.BlockSpec(memory_space=pl.ANY)] * 3,
        out_specs=pl.BlockSpec(memory_space=pltpu.VMEM),
        scratch_shapes=[
            pltpu.VMEM((2, 4, 4 * GRP, half + PAD), bf16),
            pltpu.VMEM((width, units), bf16),
            pltpu.VMEM((width, units), bf16),
            pltpu.VMEM((units, width), bf16),
            pltpu.VMEM((4 * GRP, units), bf16),
            pltpu.VMEM((4 * GRP, 1), jnp.float32),
            pltpu.VMEM((4, 4 * GRP, half), bf16),
            pltpu.VMEM((2, 4 * GRP, half), bf16),
            pltpu.VMEM((4 * GRP, half), bf16),
            pltpu.VMEM((3, GRP, half), bf16),
            dma((3,)),
            dma((3,)), dma((3,)),
            dma((4,)), dma((4,)),
            dma((2, 4)), dma((2, 4)),
            dma((4, 4)), dma((4, 4)),
            dma((4, 2)), dma((4, 2)),
            dma((2, 4)), dma((2, 4)),
            dma((4,)), dma((4,)),
            dma((3,)), dma((3,)),
        ],
        compiler_params=pltpu.CompilerParams(
            collective_id=0, has_side_effects=True, vmem_limit_bytes=63 * 1024 * 1024
        ),
        cost_estimate=pl.CostEstimate(
            flops=flops, bytes_accessed=6 * width * units, transcendentals=16 * GRP * units
        ),
    )(block, gate, up, down)


def shards(
    tokens,
    expert_ids,
    route_weights,
    gate_weight,
    up_weight,
    down_weight,
    value_weight,
    sequence_ids,
):
    tok_count, width_part = tokens.shape
    groups = lax.axis_size("ep")
    parts = lax.axis_size("tp")
    share = route_weights / jnp.sum(route_weights, axis=1, keepdims=True)
    named = expert_ids[:, :, None] == jnp.arange(groups, dtype=jnp.int32)[None, None, :]
    dense = jnp.sum(jnp.where(named, share[:, :, None], 0.0), axis=1)
    columns = []
    rest = dense
    for _ in range(3):
        top = lax.reduce_precision(rest, 8, 7)
        columns.append(top.astype(jnp.bfloat16))
        rest = rest - top
    blank = jnp.zeros((tok_count, PAD - 3 * groups), jnp.bfloat16)
    block = jnp.concatenate([tokens] + columns + [blank], axis=1)
    layer_output = routed_layer(block, gate_weight[0], up_weight[0], down_weight[0])
    return (layer_output, head(layer_output, value_weight, sequence_ids, parts))


def solution(mesh):
    in_specs = (
        P("ep", "tp"),
        P("ep", None),
        P("ep", None),
        P("ep", None, "tp"),
        P("ep", None, "tp"),
        P("ep", "tp", None),
        P("tp"),
        P("ep", None),
    )
    out_specs = (P("ep", "tp"), P("ep", None))
    body = shards if dict(mesh.shape) == {"tp": 2, "ep": 16} else plain_shards
    return jax.shard_map(body, mesh=mesh, in_specs=in_specs, out_specs=out_specs, check_vma=False)
```

```python
import functools

import jax
import jax.numpy as jnp
from jax import lax
from jax.experimental import pallas as pl
from jax.experimental.pallas import tpu as pltpu
from jax.sharding import PartitionSpec as P

SEQ_GRP = 4
CHUNKS = 1


def head(layer_output, value_weight, sequence_ids, parts):
    width_part = layer_output.shape[1]
    as_float = layer_output.astype(jnp.float32)
    squares = jnp.sum(as_float * as_float, axis=1)
    along = jnp.sum(as_float * value_weight[None, :], axis=1)
    squares, along = lax.psum((squares, along), "tp")
    values = along * lax.rsqrt(squares / (width_part * parts) + 1e-06)
    members = (sequence_ids[0][None, :] == jnp.arange(SEQ_GRP, dtype=jnp.int32)[:, None]).astype(
        jnp.float32
    )
    sums = jnp.sum(members * values[None, :], axis=1)
    counts = jnp.sum(members, axis=1)
    rewards = sums / counts
    return rewards[None, :]


def plain_shards(
    tokens,
    expert_ids,
    route_weights,
    gate_weight,
    up_weight,
    down_weight,
    value_weight,
    sequence_ids,
):
    tok_count, width_part = tokens.shape
    groups = lax.axis_size("ep")
    parts = lax.axis_size("tp")
    share = route_weights / jnp.sum(route_weights, axis=1, keepdims=True)
    named = expert_ids[:, :, None] == jnp.arange(groups, dtype=jnp.int32)[None, None, :]
    dense = jnp.sum(jnp.where(named, share[:, :, None], 0.0), axis=1)
    dense_all = lax.all_gather(dense, "ep", axis=0)
    mine = lax.dynamic_index_in_dim(dense_all, lax.axis_index("ep"), 2, keepdims=False)
    gate_local = gate_weight[0].reshape(parts, width_part, -1)
    up_local = up_weight[0].reshape(parts, width_part, -1)
    rows = tok_count // CHUNKS
    pieces = []
    for c in range(CHUNKS):
        own = tokens[c * rows:(c + 1) * rows]
        half = lax.all_gather(own, "ep", axis=0, tiled=True)
        full = lax.all_gather(half, "tp", axis=0)
        gate = jnp.einsum("qtd,qdf->tf", full, gate_local, preferred_element_type=jnp.float32)
        upper = jnp.einsum("qtd,qdf->tf", full, up_local, preferred_element_type=jnp.float32)
        scale = mine[:, c * rows:(c + 1) * rows].reshape(groups * rows, 1)
        hidden = (jax.nn.silu(gate) * upper).astype(jnp.bfloat16)
        terms = jnp.dot(hidden, down_weight[0], preferred_element_type=jnp.float32)
        terms = (terms * scale).astype(jnp.bfloat16)
        summed = lax.psum_scatter(terms, "tp", scatter_dimension=1, tiled=True)
        pieces.append(lax.psum_scatter(summed, "ep", scatter_dimension=0, tiled=True))
    routed = jnp.concatenate(pieces, axis=0).astype(jnp.float32)
    layer_output = (tokens.astype(jnp.float32) + routed).astype(jnp.bfloat16)
    return (layer_output, head(layer_output, value_weight, sequence_ids, parts))


MESH = pl.DeviceIdType.MESH
GRP = 128
PAD = 128
ORDER = (3, 0, 2, 1)


def fused(
    tok, value_row, seq, gate_hbm, up_hbm, down_hbm, out, rewards,
    held, gate_w, up_w, down_w, hid, scale, part, s_in, f_in, z_in, stats,
    w_sem, az_s, az_r, af_s, af_r, as_s, as_r, at_s, at_r,
    rt_s, rt_r, rs_s, rs_r, rf_s, rf_r, rz_s, rz_r, v_sem,
):
    half = out.shape[1]
    t = lax.axis_index("tp")
    e = lax.axis_index("ep")
    x = lax.rem(e, 2)
    y = lax.rem(lax.div(e, 2), 2)
    z = lax.div(e, 4)
    l_own = lax.rem(e, 4)
    l_x = l_own + 1 - 2 * x
    l_y = l_own + 2 - 4 * y
    l_diag = 3 - l_own
    e_x = e + 1 - 2 * x
    e_y = e + 2 - 4 * y
    e_f = e_y * (1 - t) + e_x * t
    e_s = e_x * (1 - t) + e_y * t
    l_f = l_y * (1 - t) + l_x * t
    l_s = l_x * (1 - t) + l_y * t
    lines = (l_own, l_x, l_y, l_diag)
    i_f = 2 - t
    i_s = 1 + t
    near = (t, e_f)
    far = (t, e_s)
    twin = (1 - t, e)

    def peer(d):
        return (t, lax.rem(z + d, 4) * 4 + l_own)

    def span(d):
        return pl.ds(pl.multiple_of(lax.rem(z - d + 4, 4) * GRP, GRP), GRP)

    def remote(src, dst, send, recv, target):
        return pltpu.make_async_remote_copy(
            src_ref=src, dst_ref=dst, send_sem=send, recv_sem=recv,
            device_id=target, device_id_type=MESH,
        )

    loads = [
        pltpu.make_async_copy(a, b, w_sem.at[i])
        for i, (a, b) in enumerate(((gate_hbm, gate_w), (up_hbm, up_w), (down_hbm, down_w)))
    ]
    for load in loads:
        load.start()

    barrier = pltpu.get_barrier_semaphore()
    for target in (peer(1), peer(2), peer(3), near, far, twin):
        pl.semaphore_signal(barrier, inc=1, device_id=target, device_id_type=MESH)
    pl.semaphore_wait(barrier, 6)

    def own_block(d):
        return tok if d == 0 else held.at[t, l_own, span(d)]

    def z_copy(d, step):
        k = (d + step) % 4
        return remote(
            own_block(d), held.at[t, l_own, span(d)], az_s.at[0 if step > 0 else 1, d],
            az_r.at[k - 1], peer(step % 4),
        )

    def f_copy(d):
        return remote(own_block(d), held.at[t, l_own, span(d)], af_s.at[d], af_r.at[d], near)

    def s_copy(k, d):
        line = l_own if k == 0 else l_f
        src = own_block(d) if k == 0 else held.at[t, line, span(d)]
        return remote(src, held.at[t, line, span(d)], as_s.at[k, d], as_r.at[k, d], far)

    def t_copy(i, line, d, src=None):
        src = held.at[t, line, span(d)] if src is None else src
        return remote(src, held.at[t, line, span(d)], at_s.at[i, d], at_r.at[i, d], twin)

    def arrived(line, d, sem, core=None):
        ref = held.at[t if core is None else core, line, span(d)]
        remote(ref, ref, w_sem.at[0], sem, twin).wait_recv()

    sent = []

    def go(copy):
        copy.start()
        sent.append(copy)

    pl.when(z < 3)(lambda: z_copy(0, 1).start())
    pl.when(z > 0)(lambda: z_copy(0, -1).start())
    go(f_copy(0))
    go(s_copy(0, 0))
    go(t_copy(0, l_own, 0, tok))
    held[t, l_own, span(0)] = tok[...]

    def near_block(d):
        arrived(l_f, d, af_r.at[d])
        s_copy(1, d).start()
        t_copy(i_f, l_f, d).start()

    def line_block(d, step):
        arrived(l_own, d, az_r.at[d - 1])
        if step > 0 and d < 3:
            pl.when(z < 3)(lambda: z_copy(d, 1).start())
        if step < 0 and d > 1:
            pl.when(z > 0)(lambda: z_copy(d, -1).start())
        f_copy(d).start()
        s_copy(0, d).start()
        t_copy(0, l_own, d).start()
        near_block(d)

    near_block(0)
    for hop in (1, 2, 3):
        pl.when(z >= hop)(functools.partial(line_block, hop, 1))
        pl.when(z + hop <= 3)(functools.partial(line_block, 4 - hop, -1))

    def gather_sent():
        for d in range(4):
            if d < 3:
                pl.when((z >= d) & (z < 3))(lambda d=d: z_copy(d, 1).wait_send())
            if d != 1:
                up = 0 if d == 0 else 4 - d
                pl.when((z + up <= 3) & (z > 0))(lambda d=d: z_copy(d, -1).wait_send())
            s_copy(1, d).wait_send()
            t_copy(i_f, l_f, d).wait_send()
            if d:
                f_copy(d).wait_send()
                s_copy(0, d).wait_send()
                t_copy(0, l_own, d).wait_send()

    def side(c):
        return pl.ds(c * (half // 2), half // 2)

    def rows(d):
        return pl.ds(d * GRP, GRP)

    def rs_copy(k, c, d):
        i = i_s if k == 0 else 3
        return remote(
            part.at[i, rows(d), side(c)], s_in.at[k, rows(d), side(c)],
            rs_s.at[k, c, d], rs_r.at[k, c, d], far,
        )

    def send_far(k, c):
        for d in ORDER:
            rs_copy(k, c, d).start()

    def expert(i):
        line = lines[i]
        for d in range(4):
            arrived(line, d, at_r.at[i, d], 1 - t)
        lane = lax.broadcasted_iota(jnp.int32, (4 * GRP, PAD), 1)
        shares = held[t, line, :, pl.ds(half, PAD)].astype(jnp.float32)
        scale[...] = jnp.sum(jnp.where(lax.rem(lane, 16) == e, shares, 0.0), axis=1, keepdims=True)

        def hidden(n, carry):
            cols = pl.ds(pl.multiple_of(n * 768, 768), 768)
            a = held[0, line, :, pl.ds(0, half)]
            b = held[1, line, :, pl.ds(0, half)]
            f32 = jnp.float32
            g = jnp.dot(a, gate_w[pl.ds(0, half), cols], preferred_element_type=f32)
            g += jnp.dot(b, gate_w[pl.ds(half, half), cols], preferred_element_type=f32)
            u = jnp.dot(a, up_w[pl.ds(0, half), cols], preferred_element_type=f32)
            u += jnp.dot(b, up_w[pl.ds(half, half), cols], preferred_element_type=f32)
            hid[:, cols] = (g / (1.0 + jnp.exp(-g)) * u * scale[...]).astype(jnp.bfloat16)
            return carry

        lax.fori_loop(0, hid.shape[1] // 768, hidden, 0)

        def term(n, core):
            cols = pl.ds(pl.multiple_of(core * half + n * 512, 512), 512)
            return jnp.dot(hid[...], down_w[:, cols], preferred_element_type=jnp.float32)

        def swap(c):
            return remote(
                held.at[1 - t, line, :, side(c)], part.at[i, :, side(c)],
                rt_s.at[i, c], rt_r.at[i, c], twin,
            )

        steps = half // 1024
        for c in range(2):
            def other(n, carry):
                cols = pl.ds(pl.multiple_of(n * 512, 512), 512)
                held[1 - t, line, :, cols] = term(n, 1 - t).astype(jnp.bfloat16)
                return carry

            lax.fori_loop(c * steps, (c + 1) * steps, other, 0)
            go(swap(c))
        for c in range(2):
            swap(c).wait_recv()

            def mine(n, carry):
                cols = pl.ds(pl.multiple_of(n * 512, 512), 512)
                total = term(n, t) + part[i, :, cols].astype(jnp.float32)
                part[i, :, cols] = total.astype(jnp.bfloat16)
                return carry

            lax.fori_loop(c * steps, (c + 1) * steps, mine, 0)
            if i == 3:
                send_far(1, c)
            elif i > 0:
                pl.when(t == i - 1)(functools.partial(send_far, 0, c))

    for load in loads:
        load.wait()
    expert(0)
    for d in (0, 1, 3, 2):
        arrived(l_s, d, as_r.at[0, d])
        go(t_copy(i_s, l_s, d))
    expert(1)
    for d in (0, 1, 3, 2):
        arrived(l_diag, d, as_r.at[1, d])
        go(t_copy(3, l_diag, d))
    expert(2)
    expert(3)

    def add(dst, row, c, *others):
        def chunk(r, carry):
            at = pl.ds(pl.multiple_of(row + r * 16, 16), 16)
            total = dst[at, side(c)].astype(jnp.float32)
            for other in others:
                total += other[at, side(c)].astype(jnp.float32)
            dst[at, side(c)] = total.astype(jnp.bfloat16)
            return carry

        lax.fori_loop(0, GRP // 16, chunk, 0)

    def rf_copy(c, d):
        return remote(
            part.at[i_f, rows(d), side(c)], f_in.at[rows(d), side(c)],
            rf_s.at[c, d], rf_r.at[c, d], near,
        )

    def up_copy(c, d):
        return remote(
            part.at[0, rows(d), side(c)], z_in.at[0, d - 1, :, side(c)],
            rz_s.at[0, c, d], rz_r.at[0, c, d], peer(1),
        )

    def down_copy(c, d):
        return remote(
            part.at[0, rows(d), side(c)], z_in.at[1, d, :, side(c)],
            rz_s.at[1, c, d], rz_r.at[1, c, d], peer(3),
        )

    def join(way, copy, c, d):
        copy(c, d).wait_recv()
        slot = d - 1 if way == 0 else d

        def chunk(r, carry):
            at = pl.ds(pl.multiple_of(d * GRP + r * 16, 16), 16)
            came = z_in[way, slot, pl.ds(pl.multiple_of(r * 16, 16), 16), side(c)]
            total = part[0, at, side(c)].astype(jnp.float32) + came.astype(jnp.float32)
            part[0, at, side(c)] = total.astype(jnp.bfloat16)
            return carry

        lax.fori_loop(0, GRP // 16, chunk, 0)

    def line_step(c, d):
        def up():
            pl.when(z > 0)(lambda: join(0, up_copy, c, d))
            up_copy(c, d).start()

        def down():
            pl.when(z < 3)(lambda: join(1, down_copy, c, d))
            down_copy(c, d).start()

        if d > 0:
            pl.when(z < d)(up)
        if d < 3:
            pl.when(z > d)(down)

    def line_end(c, d):
        def mine():
            if d > 0:
                join(0, up_copy, c, d)
            if d < 3:
                join(1, down_copy, c, d)

        pl.when(z == d)(mine)

    units = [(c, d) for c in range(2) for d in ORDER]
    for turn in range(len(units) + 1):
        if turn < len(units):
            c, d = units[turn]
            rs_copy(1, c, d).wait_recv()
            add(part.at[i_f], d * GRP, c, s_in.at[1])
            go(rf_copy(c, d))
        if turn > 0:
            c, d = units[turn - 1]
            rs_copy(0, c, d).wait_recv()
            rf_copy(c, d).wait_recv()
            add(part.at[0], d * GRP, c, s_in.at[0], f_in)
            line_step(c, d)
    for c, d in units:
        line_end(c, d)

    def line_sent():
        for c, d in units:
            if d > 0:
                pl.when(z < d)(lambda c=c, d=d: up_copy(c, d).wait_send())
            if d < 3:
                pl.when(z > d)(lambda c=c, d=d: down_copy(c, d).wait_send())

    def last(r, carry):
        at = pl.ds(pl.multiple_of(r * 16, 16), 16)
        total = part[0, pl.ds(pl.multiple_of(z * GRP + r * 16, 16), 16)].astype(jnp.float32)
        total += tok[at, pl.ds(0, half)].astype(jnp.float32)
        rounded = total.astype(jnp.bfloat16)
        out[at] = rounded
        as_float = rounded.astype(jnp.float32)
        squares = jnp.sum(as_float * as_float, axis=1, keepdims=True)
        along = jnp.sum(as_float * value_row[...], axis=1, keepdims=True)
        lane = lax.broadcasted_iota(jnp.int32, (16, PAD), 1)
        stats[0, at] = jnp.where(lane == 0, squares, along)
        return carry

    lax.fori_loop(0, GRP // 16, last, 0)
    trade = remote(stats.at[0], stats.at[1], v_sem.at[0], v_sem.at[1], twin)
    trade.start()
    for copy in sent:
        copy.wait_send()
    gather_sent()
    line_sent()
    for k in range(2):
        for c in range(2):
            for d in range(4):
                rs_copy(k, c, d).wait_send()
    trade.wait()
    both = stats[0] + stats[1]
    values = both[:, 1:2] * lax.rsqrt(both[:, 0:1] / (2 * half) + 1e-06)
    lane = lax.broadcasted_iota(jnp.int32, (GRP, PAD), 1)
    members = (seq[...] == lane).astype(jnp.float32)
    sums = jnp.sum(members * values, axis=0, keepdims=True)
    counts = jnp.sum(members, axis=0, keepdims=True)
    rewards[...] = sums / jnp.maximum(counts, 1.0)


def routed_layer(block, value_row, seq, gate, up, down):
    half = block.shape[1] - PAD
    width, units = gate.shape
    bf16 = jnp.bfloat16
    dma = pltpu.SemaphoreType.DMA
    flops = 2 * 16 * GRP * 3 * width * units
    return pl.pallas_call(
        fused,
        out_shape=(
            jax.ShapeDtypeStruct((GRP, half), bf16),
            jax.ShapeDtypeStruct((1, PAD), jnp.float32),
        ),
        in_specs=[pl.BlockSpec(memory_space=pltpu.VMEM)] * 3 + [pl.BlockSpec(memory_space=pl.ANY)] * 3,
        out_specs=(pl.BlockSpec(memory_space=pltpu.VMEM),) * 2,
        scratch_shapes=[
            pltpu.VMEM((2, 4, 4 * GRP, half + PAD), bf16),
            pltpu.VMEM((width, units), bf16),
            pltpu.VMEM((width, units), bf16),
            pltpu.VMEM((units, width), bf16),
            pltpu.VMEM((4 * GRP, units), bf16),
            pltpu.VMEM((4 * GRP, 1), jnp.float32),
            pltpu.VMEM((4, 4 * GRP, half), bf16),
            pltpu.VMEM((2, 4 * GRP, half), bf16),
            pltpu.VMEM((4 * GRP, half), bf16),
            pltpu.VMEM((2, 3, GRP, half), bf16),
            pltpu.VMEM((2, GRP, PAD), jnp.float32),
            dma((3,)),
            dma((2, 4)), dma((3,)),
            dma((4,)), dma((4,)),
            dma((2, 4)), dma((2, 4)),
            dma((4, 4)), dma((4, 4)),
            dma((4, 2)), dma((4, 2)),
            dma((2, 2, 4)), dma((2, 2, 4)),
            dma((2, 4)), dma((2, 4)),
            dma((2, 2, 4)), dma((2, 2, 4)),
            dma((2,)),
        ],
        compiler_params=pltpu.CompilerParams(
            collective_id=0, has_side_effects=True, vmem_limit_bytes=63 * 1024 * 1024
        ),
        cost_estimate=pl.CostEstimate(
            flops=flops, bytes_accessed=6 * width * units, transcendentals=16 * GRP * units
        ),
    )(block, value_row, seq, gate, up, down)


def shards(
    tokens,
    expert_ids,
    route_weights,
    gate_weight,
    up_weight,
    down_weight,
    value_weight,
    sequence_ids,
):
    tok_count, width_part = tokens.shape
    groups = lax.axis_size("ep")
    share = route_weights / jnp.sum(route_weights, axis=1, keepdims=True)
    named = expert_ids[:, :, None] == jnp.arange(groups, dtype=jnp.int32)[None, None, :]
    dense = jnp.sum(jnp.where(named, share[:, :, None], 0.0), axis=1)
    columns = []
    rest = dense
    for _ in range(3):
        top = lax.reduce_precision(rest, 8, 7)
        columns.append(top.astype(jnp.bfloat16))
        rest = rest - top
    blank = jnp.zeros((tok_count, PAD - 3 * groups), jnp.bfloat16)
    block = jnp.concatenate([tokens] + columns + [blank], axis=1)
    layer_output, rewards = routed_layer(
        block, value_weight[None, :], sequence_ids.reshape(tok_count, 1),
        gate_weight[0], up_weight[0], down_weight[0],
    )
    return (layer_output, rewards[:, :SEQ_GRP])


def solution(mesh):
    in_specs = (
        P("ep", "tp"),
        P("ep", None),
        P("ep", None),
        P("ep", None, "tp"),
        P("ep", None, "tp"),
        P("ep", "tp", None),
        P("tp"),
        P("ep", None),
    )
    out_specs = (P("ep", "tp"), P("ep", None))
    body = shards if dict(mesh.shape) == {"tp": 2, "ep": 16} else plain_shards
    return jax.shard_map(body, mesh=mesh, in_specs=in_specs, out_specs=out_specs, check_vma=False)
```
